32 devices in a mesh: section: 4 (over y, x), seq: 8 (over z, core).
Axes of the slice: x: 2, y: 2, z: 4, core: 2. Of those that a mesh axis runs over, the one named last changes fastest.
Arguments:
- hidden: bfloat16 [4, 1024, 2048], P('section', 'seq'), may hold values from -6 to 6
- query_gain: bfloat16 [4, 2048], P('section'), may hold values from 0.099609375 to 1.8984375
- out_gain: bfloat16 [4, 2048], P('section'), may hold values from 0.099609375 to 1.8984375
- keys_now: bfloat16 [4, 1024, 512], P('section', 'seq'), may hold values from -26.516504 to 26.516504
- values_now: bfloat16 [4, 1024, 512], P('section', 'seq'), may hold values from -6 to 6
- keys_cached: bfloat16 [4, 1024, 512], P('section', 'seq'), may hold values from -6 to 6
- values_cached: bfloat16 [4, 1024, 512], P('section', 'seq'), may hold values from -6 to 6
- first_key: int32 [4], P('section'), may hold values from 0 to 1024
Outputs:
- handoff: bfloat16 [4, 1024, 2048], P('section', 'seq')
The draws below stay inside these ranges and needn't reach their ends.
All inputs are finite; a program needn't handle non-finite values.
Results may differ from the reference program's by a relative error of at most 0.0065.
Values may be sent and summed in bfloat16 or wider, within the bound.
A program may use at most 128 MiB of HBM per device.

```python
import jax
import jax.numpy as jnp
from jax import lax

HEADS = 16
KV_HEADS = 4
HEAD = 128
SECTIONS = 4
STRETCH = 1024


def drawn(key):
    hidden_draw = jax.random.truncated_normal(jax.random.fold_in(key, 101), -6.0, 6.0, (SECTIONS, STRETCH, HEADS * HEAD), jnp.float32)
    keys_draw = jax.random.truncated_normal(jax.random.fold_in(key, 102), -6.0, 6.0, (SECTIONS, STRETCH, KV_HEADS * HEAD), jnp.float32)
    return (hidden_draw, keys_draw)


def draw_hidden(key, part):
    return drawn(key)[0].astype(jnp.bfloat16)


def draw_keys_now(key, part):
    return drawn(key)[1].astype(jnp.bfloat16)


def plant(values, key, smallest, top_value):
    place = [jax.random.randint(jax.random.fold_in(key, axis), (), 0, length) for axis, length in enumerate(values.shape)]
    widest = values.shape.index(max(values.shape))
    neighbour = place[:widest] + [(place[widest] + 1) % values.shape[widest]] + place[widest + 1:]
    return values.at[tuple(place)].set(smallest).at[tuple(neighbour)].set(top_value)


def steps_of(key, extent, cuts, least, largest):
    level = 1.0
    for position, shards_of in cuts:
        steps = jax.random.uniform(jax.random.fold_in(jax.random.fold_in(key, 6), position), (shards_of,), jnp.float32, least / len(cuts), largest / len(cuts))
        level = level * jnp.repeat(jnp.exp(steps), extent[position] // shards_of).reshape((-1,) + (1,) * (len(extent) - 1 - position))
    return level


def scatter_about(rng, extent, spread, reach, pieces=(), kind=jnp.bfloat16):
    values = spread * jax.random.normal(rng, extent, jnp.float32)
    if pieces:
        values = values * steps_of(rng, extent, pieces, -0.22, 0.18)
    return jnp.clip(values, -reach, reach).astype(kind)


def setup_inputs(seed: int = 0) -> dict:
    streams_of = jax.random.split(jax.random.key(seed), 9)
    hidden = draw_hidden(jax.random.fold_in(streams_of[8], 71), 0)
    query_gain = jnp.clip(1.0 + 0.18 * jax.random.normal(streams_of[1], (SECTIONS, HEADS * HEAD), jnp.float32), 0.099609375, 1.8984375).astype(jnp.bfloat16)
    out_gain = jnp.clip(1.0 + 0.18 * jax.random.normal(streams_of[2], (SECTIONS, HEADS * HEAD), jnp.float32), 0.099609375, 1.8984375).astype(jnp.bfloat16)
    keys_now = draw_keys_now(jax.random.fold_in(streams_of[8], 71), 0)
    values_now = scatter_about(streams_of[4], (SECTIONS, STRETCH, KV_HEADS * HEAD), 1.0, 6.0, ((0, 4), (1, 8)))
    keys_cached = scatter_about(streams_of[5], (SECTIONS, STRETCH, KV_HEADS * HEAD), 1.0, 6.0, ((0, 4), (1, 8)))
    values_cached = scatter_about(streams_of[6], (SECTIONS, STRETCH, KV_HEADS * HEAD), 1.0, 6.0, ((0, 4), (1, 8)))
    first_key = plant(jax.random.randint(streams_of[7], (SECTIONS,), 0, STRETCH + 1), jax.random.fold_in(streams_of[7], 1), 0, STRETCH).astype(jnp.int32)
    return dict(hidden=hidden, query_gain=query_gain, out_gain=out_gain, keys_now=keys_now, values_now=values_now, keys_cached=keys_cached, values_cached=values_cached, first_key=first_key)


masked_score = -1e+30

def rms_scale(values):
    return lax.rsqrt(lax.optimization_barrier(jnp.mean(values * values, axis=-1, keepdims=True)) + 1e-06)

def one_section(inputs):
    hidden, query_gain, out_gain, keys_now, values_now, keys_cached, values_cached, first_key = inputs
    widened = hidden.astype(jnp.float32)
    queries = (widened * rms_scale(widened) * query_gain.astype(jnp.float32)).astype(jnp.bfloat16)
    grouped = queries.reshape(STRETCH, KV_HEADS, HEADS // KV_HEADS, HEAD)
    all_keys = jnp.concatenate([keys_cached, keys_now], 0).reshape(2 * STRETCH, KV_HEADS, HEAD)
    all_values = jnp.concatenate([values_cached, values_now], 0).reshape(2 * STRETCH, KV_HEADS, HEAD)
    block_rows = min(512, STRETCH)
    score_scale = HEAD ** (-0.5)

    def attend(block_start):
        query_block = lax.dynamic_slice_in_dim(grouped, block_start, block_rows, 0)
        key_block = lax.dynamic_slice_in_dim(all_keys, block_start, STRETCH + block_rows, 0)
        value_block = lax.dynamic_slice_in_dim(all_values, block_start, STRETCH + block_rows, 0)
        scores = jnp.einsum('tgqd,bgd->gqtb', query_block.astype(jnp.float32), key_block.astype(jnp.float32)) * score_scale
        positions = block_start + jnp.arange(block_rows, dtype=jnp.int32)
        columns = block_start + jnp.arange(STRETCH + block_rows, dtype=jnp.int32)
        visible = (columns[None, :] > positions[:, None]) & (columns[None, :] <= positions[:, None] + STRETCH) & (columns[None, :] >= first_key)
        scores = jnp.where(visible, scores, masked_score)
        highest = lax.optimization_barrier(jnp.max(scores, axis=-1, keepdims=True))
        weights = jnp.exp(scores - highest)
        totals = lax.optimization_barrier(jnp.sum(weights, axis=-1))
        rounded = lax.optimization_barrier(weights.astype(jnp.bfloat16)).astype(jnp.float32)
        summed = jnp.einsum('gqtb,bgd->gqtd', rounded, value_block.astype(jnp.float32))
        attended = (summed / totals[..., None]).astype(jnp.bfloat16)
        return jnp.transpose(attended, (2, 0, 1, 3)).reshape(block_rows, HEADS * HEAD)
    starts = (jnp.arange(STRETCH // block_rows) * block_rows).astype(jnp.int32)
    attended = lax.map(attend, starts).reshape(STRETCH, HEADS * HEAD).astype(jnp.float32)
    branch = attended * rms_scale(attended) * out_gain.astype(jnp.float32)
    return (widened + branch).astype(jnp.bfloat16)

def reference(hidden, query_gain, out_gain, keys_now, values_now, keys_cached, values_cached, first_key):
    layered = lax.map(one_section, (hidden, query_gain, out_gain, keys_now, values_now, keys_cached, values_cached, first_key))
    return jnp.roll(layered, 1, axis=0)
```

```python
import functools
import math

import jax
import jax.numpy as jnp
from jax import lax
from jax.experimental import pallas as pl
from jax.experimental.pallas import tpu as pltpu
from jax.sharding import PartitionSpec as P

HEAD = 128
EPS = 1e-06
masked_score = -1e30
MESH = pl.DeviceIdType.MESH


def kernel(
    sections,
    seq_count,
    groups,
    first_key_ref,
    hidden_ref,
    query_gain_ref,
    out_gain_ref,
    keys_now_ref,
    values_now_ref,
    keys_cached_ref,
    values_cached_ref,
    out_ref,
    now_own,
    cached_own,
    arrived,
    hidden_own,
    query_gain,
    out_gain,
    queries_t,
    highest,
    totals,
    weighted,
    attended_own,
    final_own,
    scale_own,
    hidden_in,
    gain_in,
    attended_in,
    final_in,
    scale_in,
    squares,
    local_sem,
    arrive_sem,
    chain_sem,
    partner_sem,
    section_send,
    section_recv,
):
    rows, width = hidden_ref.shape
    group_width = width // groups
    heads_in_group = group_width // HEAD
    chips = seq_count // 2
    early = group_width * (groups - 1)
    factor = math.log2(math.e) * HEAD ** (-0.5)
    section = lax.axis_index("section")
    me = lax.axis_index("seq")
    chip = lax.div(me, 2)
    core = lax.rem(me, 2)
    partner = me + 1 - 2 * core
    next_section = lax.rem(section + 1, sections)
    last_section = lax.rem(section + sections - 1, sections)
    limit = first_key_ref[0]

    hidden_copy = pltpu.make_async_copy(hidden_ref, hidden_own, local_sem.at[0])
    gain_copy = pltpu.make_async_copy(query_gain_ref, query_gain, local_sem.at[1])
    out_gain_copy = pltpu.make_async_copy(out_gain_ref, out_gain, local_sem.at[2])
    pieces = []
    for group in range(groups):
        columns = pl.ds(group * HEAD, HEAD)
        pieces.append(
            [
                pltpu.make_async_copy(
                    source.at[:, columns],
                    packed.at[group, :, pl.ds(half * HEAD, HEAD)],
                    local_sem.at[3 + 4 * group + number],
                )
                for number, (source, packed, half) in enumerate(
                    (
                        (keys_now_ref, now_own, 0),
                        (values_now_ref, now_own, 1),
                        (keys_cached_ref, cached_own, 0),
                        (values_cached_ref, cached_own, 1),
                    )
                )
            ]
        )
    for copy in pieces[0]:
        copy.start()
    hidden_copy.start()
    gain_copy.start()
    out_gain_copy.start()
    for group in range(1, groups):
        for copy in pieces[group]:
            copy.start()

    barrier = pltpu.get_barrier_semaphore()

    def greet(section_id, seq_id):
        pl.semaphore_signal(barrier, inc=1, device_id=(section_id, seq_id), device_id_type=MESH)

    greet(section, partner)
    greet(next_section, me)
    greet(last_section, me)

    @pl.when(chip > 0)
    def _():
        greet(section, me - 2)

    @pl.when(chip < chips - 1)
    def _():
        greet(section, me + 2)

    ends = (chip == 0).astype(jnp.int32) + (chip == chips - 1).astype(jnp.int32)
    pl.semaphore_wait(barrier, 5 - ends)

    def along(source, owner, group, send_sem, target):
        return pltpu.make_async_remote_copy(
            src_ref=source,
            dst_ref=arrived.at[owner, group],
            send_sem=send_sem,
            recv_sem=arrive_sem.at[owner, group],
            device_id=(section, target),
            device_id_type=MESH,
        )

    def to_next(source, target, number):
        return pltpu.make_async_remote_copy(
            src_ref=source,
            dst_ref=target,
            send_sem=section_send.at[number],
            recv_sem=section_recv.at[number],
            device_id=(next_section, me),
            device_id_type=MESH,
        )

    hidden_send = to_next(hidden_ref.at[:, pl.ds(0, early)], hidden_in, groups)
    gain_send = to_next(out_gain, gain_in, groups + 1)
    scale_send = to_next(scale_own, scale_in, groups + 2)
    final_send = to_next(final_own, final_in, groups - 1)

    def attended_send(group):
        return to_next(attended_own.at[group], attended_in.at[group], group)

    for group in range(groups):
        for copy in pieces[group]:
            copy.wait()

        @pl.when(chip < chips - 1)
        def _():
            along(now_own.at[group], me, group, chain_sem.at[chip, group], me + 2).start()

        @pl.when(chip > 0)
        def _():
            along(cached_own.at[group], me, group, chain_sem.at[chips, group], me - 2).start()

        @pl.when(core == 0)
        def _():
            along(now_own.at[group], me, group, partner_sem.at[chip, group], partner).start()

        @pl.when(core == 1)
        def _():
            along(cached_own.at[group], me, group, partner_sem.at[chip, group], partner).start()

        if group == 0:
            hidden_send.start()
            out_gain_copy.wait()
            gain_send.start()

    hidden_copy.wait()
    gain_copy.wait()
    widened = hidden_own[...].astype(jnp.float32)
    scale = lax.rsqrt(jnp.mean(widened * widened, axis=-1, keepdims=True) + EPS)
    for head in range(groups * heads_in_group):
        columns = slice(head * HEAD, (head + 1) * HEAD)
        queries = (
            hidden_own[:, columns].astype(jnp.float32)
            * scale
            * query_gain[:, columns].astype(jnp.float32)
        )
        place = head % heads_in_group
        queries_t[head // heads_in_group, :, place * rows : (place + 1) * rows] = (
            queries.T.astype(jnp.bfloat16)
        )

    def scored(keys, group):
        return jnp.dot(keys, queries_t[group], preferred_element_type=jnp.float32)

    def summed(values, weights):
        return lax.dot_general(
            values,
            weights.astype(jnp.bfloat16),
            (((0,), (0,)), ((), ())),
            preferred_element_type=jnp.float32,
        )

    def absorb(scores, values, group):
        old = highest[group]
        new = jnp.maximum(old, jnp.max(scores, axis=0, keepdims=True))
        rescale = jnp.exp2((old - new) * factor)
        weights = jnp.exp2((scores - new) * factor)
        highest[group] = new
        totals[group] = totals[group] * rescale + jnp.sum(weights, axis=0, keepdims=True)
        weighted[group] = weighted[group] * rescale + summed(values, weights)

    def own_part(group, _):
        key_pos = lax.broadcasted_iota(jnp.int32, (rows, group_width // HEAD * rows), 0)
        query_pos = lax.rem(
            lax.broadcasted_iota(jnp.int32, (rows, group_width // HEAD * rows), 1), rows
        )
        scores = jnp.where(
            key_pos <= query_pos, scored(now_own[group, :, :HEAD], group), masked_score
        )
        new = jnp.max(scores, axis=0, keepdims=True)
        weights = jnp.exp2((scores - new) * factor)
        highest[group] = new
        totals[group] = jnp.sum(weights, axis=0, keepdims=True)
        weighted[group] = summed(now_own[group, :, HEAD:], weights)
        scores = jnp.where(
            (key_pos > query_pos) & (key_pos + me * rows >= limit),
            scored(cached_own[group, :, :HEAD], group),
            masked_score,
        )
        absorb(scores, cached_own[group, :, HEAD:], group)
        along(arrived.at[partner, group], partner, group, partner_sem.at[chip, group], partner).wait_recv()
        bound = jnp.where(partner > me, limit, 0)
        scores = jnp.where(
            key_pos + partner * rows >= bound,
            scored(arrived[partner, group, :, :HEAD], group),
            masked_score,
        )
        absorb(scores, arrived[partner, group, :, HEAD:], group)
        return 0

    lax.fori_loop(0, groups, own_part, 0)

    others = chips - 1
    both = jnp.minimum(chip, others - chip)

    def visited(step):
        group = lax.div(step, others)
        order = lax.rem(step, others) + 1
        paired = order <= 2 * both
        distance = jnp.where(paired, lax.div(order + 1, 2), order - both)
        lower = jnp.where(paired, lax.rem(order, 2) == 1, chip > both)
        return group, chip + jnp.where(lower, -distance, distance), lower

    def relay(step):
        group, other, lower = visited(step)
        owner = 2 * other + core
        block = arrived.at[owner, group]
        along(block, owner, group, chain_sem.at[other, group], partner).wait_recv()

        @pl.when(lower & (chip < chips - 1))
        def _():
            along(block, owner, group, chain_sem.at[other, group], me + 2).start()

        @pl.when(jnp.logical_not(lower) & (chip > 0))
        def _():
            along(block, owner, group, chain_sem.at[other, group], me - 2).start()

        along(block, owner, group, partner_sem.at[other, group], partner).start()

    def fold(step):
        group, other, lower = visited(step)
        owner = 2 * other + 1 - core
        block = arrived.at[owner, group]
        along(block, owner, group, chain_sem.at[other, group], partner).wait_recv()
        first = pl.multiple_of(2 * other, 2)
        both_blocks = arrived[pl.ds(first, 2), group].reshape(2 * rows, 2 * HEAD)
        key_pos = lax.broadcasted_iota(jnp.int32, (2 * rows, 1), 0) + first * rows
        bound = jnp.where(lower, 0, limit)
        scores = jnp.where(key_pos >= bound, scored(both_blocks[:, :HEAD], group), masked_score)
        absorb(scores, both_blocks[:, HEAD:], group)

    squares[...] = jnp.zeros_like(squares)

    def closed(group):
        attended_t = (weighted[group] / totals[group]).astype(jnp.bfloat16).astype(jnp.float32)
        row_squares = jnp.sum(attended_t * attended_t, axis=0, keepdims=True)
        for head in range(heads_in_group):
            squares[...] += row_squares[:, head * rows : (head + 1) * rows]
        return [
            attended_t[:, head * rows : (head + 1) * rows].T for head in range(heads_in_group)
        ]

    def one_step(step, _):
        relay(step)
        fold(step - 1)
        group = lax.div(step, others)

        @pl.when(lax.rem(step, others) == 0)
        def _():
            for head, value in enumerate(closed(group - 1)):
                attended_own[group - 1, :, head * HEAD : (head + 1) * HEAD] = value.astype(
                    jnp.bfloat16
                )
            attended_send(group - 1).start()

        return 0

    steps = groups * others
    relay(0)
    lax.fori_loop(1, steps, one_step, 0)
    fold(steps - 1)

    last = closed(groups - 1)
    row_scale = lax.rsqrt(squares[...] * (1.0 / width) + EPS)
    scale_own[...] = jnp.broadcast_to(row_scale, scale_own.shape)
    scale_send.start()
    row_scale = jnp.broadcast_to(row_scale, (HEAD, rows)).T
    for head, value in enumerate(last):
        columns = slice(early + head * HEAD, early + (head + 1) * HEAD)
        branch = value * row_scale * out_gain[:, columns].astype(jnp.float32)
        final_own[:, head * HEAD : (head + 1) * HEAD] = (
            hidden_own[:, columns].astype(jnp.float32) + branch
        ).astype(jnp.bfloat16)
    final_send.start()

    hidden_send.wait_recv()
    gain_send.wait_recv()
    for group in range(groups - 1):
        attended_send(group).wait_recv()
    scale_send.wait_recv()
    row_scale = jnp.broadcast_to(scale_in[0:1, :], (HEAD, rows)).T
    for group in range(groups - 1):
        for head in range(heads_in_group):
            start = group * group_width + head * HEAD
            columns = slice(start, start + HEAD)
            branch = (
                attended_in[group, :, head * HEAD : (head + 1) * HEAD].astype(jnp.float32)
                * row_scale
                * gain_in[:, columns].astype(jnp.float32)
            )
            out_ref[:, columns] = (
                hidden_in[:, columns].astype(jnp.float32) + branch
            ).astype(jnp.bfloat16)
    final_send.wait_recv()
    out_ref[:, early:] = final_in[...]

    hidden_send.wait_send()
    gain_send.wait_send()
    scale_send.wait_send()
    final_send.wait_send()
    for group in range(groups - 1):
        attended_send(group).wait_send()

    def drained(step, _):
        group, other, lower = visited(step)
        owner = 2 * other + core
        block = arrived.at[owner, group]

        @pl.when((lower & (chip < chips - 1)) | (jnp.logical_not(lower) & (chip > 0)))
        def _():
            along(block, owner, group, chain_sem.at[other, group], partner).wait_send()

        along(block, owner, group, partner_sem.at[other, group], partner).wait_send()
        return 0

    lax.fori_loop(0, steps, drained, 0)
    for group in range(groups):

        @pl.when(chip < chips - 1)
        def _():
            along(now_own.at[group], me, group, chain_sem.at[chip, group], partner).wait_send()

        @pl.when(chip > 0)
        def _():
            along(cached_own.at[group], me, group, chain_sem.at[chips, group], partner).wait_send()

        along(now_own.at[group], me, group, partner_sem.at[chip, group], partner).wait_send()


def solution(mesh):
    sections, seq_count = mesh.shape["section"], mesh.shape["seq"]

    def on_device(
        hidden, query_gain, out_gain, keys_now, values_now, keys_cached, values_cached, first_key
    ):
        _, rows, width = hidden.shape
        groups = keys_now.shape[-1] // HEAD
        group_width = width // groups
        query_rows = group_width // HEAD * rows
        chips = seq_count // 2
        half, full = jnp.bfloat16, jnp.float32
        anywhere = pl.BlockSpec(memory_space=pl.ANY)
        result = pl.pallas_call(
            functools.partial(kernel, sections, seq_count, groups),
            out_shape=jax.ShapeDtypeStruct((rows, width), half),
            in_specs=[pl.BlockSpec(memory_space=pltpu.SMEM)] + [anywhere] * 7,
            out_specs=pl.BlockSpec(memory_space=pltpu.VMEM),
            scratch_shapes=[
                pltpu.VMEM((groups, rows, 2 * HEAD), half),
                pltpu.VMEM((groups, rows, 2 * HEAD), half),
                pltpu.VMEM((seq_count, groups, rows, 2 * HEAD), half),
                pltpu.VMEM((rows, width), half),
                pltpu.VMEM((1, width), half),
                pltpu.VMEM((1, width), half),
                pltpu.VMEM((groups, HEAD, query_rows), half),
                pltpu.VMEM((groups, 1, query_rows), full),
                pltpu.VMEM((groups, 1, query_rows), full),
                pltpu.VMEM((groups, HEAD, query_rows), full),
                pltpu.VMEM((groups - 1, rows, group_width), half),
                pltpu.VMEM((rows, group_width), half),
                pltpu.VMEM((8, rows), full),
                pltpu.VMEM((rows, width - group_width), half),
                pltpu.VMEM((1, width), half),
                pltpu.VMEM((groups - 1, rows, group_width), half),
                pltpu.VMEM((rows, group_width), half),
                pltpu.VMEM((8, rows), full),
                pltpu.VMEM((1, rows), full),
                pltpu.SemaphoreType.DMA((3 + 4 * groups,)),
                pltpu.SemaphoreType.DMA((seq_count, groups)),
                pltpu.SemaphoreType.DMA((chips + 1, groups)),
                pltpu.SemaphoreType.DMA((chips, groups)),
                pltpu.SemaphoreType.DMA((groups + 3,)),
                pltpu.SemaphoreType.DMA((groups + 3,)),
            ],
            compiler_params=pltpu.CompilerParams(collective_id=0, has_side_effects=True),
        )(
            first_key,
            hidden[0],
            query_gain,
            out_gain,
            keys_now[0],
            values_now[0],
            keys_cached[0],
            values_cached[0],
        )
        return result[None]

    return jax.shard_map(
        on_device,
        mesh=mesh,
        in_specs=(
            P("section", "seq", None),
            P("section", None),
            P("section", None),
            P("section", "seq", None),
            P("section", "seq", None),
            P("section", "seq", None),
            P("section", "seq", None),
            P("section"),
        ),
        out_specs=P("section", "seq", None),
        check_vma=False,
    )
```

```python
import functools
import math

import jax
import jax.numpy as jnp
from jax import lax
from jax.experimental import pallas as pl
from jax.experimental.pallas import tpu as pltpu
from jax.sharding import PartitionSpec as P

HEAD = 128
EPS = 1e-06
AHEAD = 2
ROOM = 20 << 20
masked_score = -1e30
MESH = pl.DeviceIdType.MESH


def kernel(
    sections,
    seq_count,
    groups,
    first_key_ref,
    hidden_ref,
    query_gain_ref,
    out_gain_ref,
    keys_now_ref,
    values_now_ref,
    keys_cached_ref,
    values_cached_ref,
    out_ref,
    now_own,
    cached_own,
    arrived,
    hidden_own,
    query_gain,
    out_gain,
    queries_t,
    highest,
    totals,
    weighted,
    attended_own,
    final_own,
    scale_own,
    hidden_in,
    gain_in,
    attended_in,
    final_in,
    scale_in,
    squares,
    local_sem,
    arrive_sem,
    chain_sem,
    partner_sem,
    section_send,
    section_recv,
):
    rows, width = hidden_ref.shape
    group_width = width // groups
    heads_in_group = group_width // HEAD
    chips = seq_count // 2
    early = group_width * (groups - 1)
    factor = math.log2(math.e) * HEAD ** (-0.5)
    section = lax.axis_index("section")
    me = lax.axis_index("seq")
    chip = lax.div(me, 2)
    core = lax.rem(me, 2)
    partner = me + 1 - 2 * core
    next_section = lax.rem(section + 1, sections)
    last_section = lax.rem(section + sections - 1, sections)
    limit = first_key_ref[0]

    hidden_copy = pltpu.make_async_copy(hidden_ref, hidden_own, local_sem.at[0])
    gain_copy = pltpu.make_async_copy(query_gain_ref, query_gain, local_sem.at[1])
    out_gain_copy = pltpu.make_async_copy(out_gain_ref, out_gain, local_sem.at[2])
    pieces = []
    for group in range(groups):
        columns = pl.ds(group * HEAD, HEAD)
        pieces.append(
            [
                pltpu.make_async_copy(
                    source.at[:, columns],
                    packed.at[group, :, pl.ds(half * HEAD, HEAD)],
                    local_sem.at[3 + 4 * group + number],
                )
                for number, (source, packed, half) in enumerate(
                    (
                        (keys_now_ref, now_own, 0),
                        (values_now_ref, now_own, 1),
                        (keys_cached_ref, cached_own, 0),
                        (values_cached_ref, cached_own, 1),
                    )
                )
            ]
        )
    for copy in pieces[0]:
        copy.start()
    hidden_copy.start()
    gain_copy.start()
    out_gain_copy.start()
    for group in range(1, groups):
        for copy in pieces[group]:
            copy.start()

    barrier = pltpu.get_barrier_semaphore()

    def greet(section_id, seq_id):
        pl.semaphore_signal(barrier, inc=1, device_id=(section_id, seq_id), device_id_type=MESH)

    greet(section, partner)
    greet(next_section, me)
    greet(last_section, me)

    @pl.when(chip > 0)
    def _():
        greet(section, me - 2)

    @pl.when(chip < chips - 1)
    def _():
        greet(section, me + 2)

    ends = (chip == 0).astype(jnp.int32) + (chip == chips - 1).astype(jnp.int32)
    pl.semaphore_wait(barrier, 5 - ends)

    def along(source, owner, group, send_sem, target):
        return pltpu.make_async_remote_copy(
            src_ref=source,
            dst_ref=arrived.at[owner, group],
            send_sem=send_sem,
            recv_sem=arrive_sem.at[owner, group],
            device_id=(section, target),
            device_id_type=MESH,
        )

    def to_next(source, target, number):
        return pltpu.make_async_remote_copy(
            src_ref=source,
            dst_ref=target,
            send_sem=section_send.at[number],
            recv_sem=section_recv.at[number],
            device_id=(next_section, me),
            device_id_type=MESH,
        )

    hidden_send = to_next(hidden_ref.at[:, pl.ds(0, early)], hidden_in, groups)
    gain_send = to_next(out_gain, gain_in, groups + 1)
    scale_send = to_next(scale_own, scale_in, groups + 2)
    final_send = to_next(final_own, final_in, groups - 1)

    def attended_send(group):
        return to_next(attended_own.at[group], attended_in.at[group], group)

    for group in range(groups):
        for copy in pieces[group]:
            copy.wait()

        @pl.when(chip < chips - 1)
        def _():
            along(now_own.at[group], me, group, chain_sem.at[chip, group], me + 2).start()

        @pl.when(chip > 0)
        def _():
            along(cached_own.at[group], me, group, chain_sem.at[chips, group], me - 2).start()

        @pl.when(core == 0)
        def _():
            along(now_own.at[group], me, group, partner_sem.at[chip, group], partner).start()

        @pl.when(core == 1)
        def _():
            along(cached_own.at[group], me, group, partner_sem.at[chip, group], partner).start()

        if group == 0:
            hidden_send.start()
            out_gain_copy.wait()
            gain_send.start()

    hidden_copy.wait()
    gain_copy.wait()
    widened = hidden_own[...].astype(jnp.float32)
    scale = lax.rsqrt(jnp.mean(widened * widened, axis=-1, keepdims=True) + EPS)
    for head in range(groups * heads_in_group):
        columns = slice(head * HEAD, (head + 1) * HEAD)
        queries = (
            hidden_own[:, columns].astype(jnp.float32)
            * scale
            * query_gain[:, columns].astype(jnp.float32)
        )
        place = head % heads_in_group
        queries_t[head // heads_in_group, :, place * rows : (place + 1) * rows] = (
            queries.T.astype(jnp.bfloat16)
        )

    def scored(keys, group):
        return jnp.dot(keys, queries_t[group], preferred_element_type=jnp.float32)

    def summed(values, weights):
        return lax.dot_general(
            values,
            weights.astype(jnp.bfloat16),
            (((0,), (0,)), ((), ())),
            preferred_element_type=jnp.float32,
        )

    def absorb(scores, values, group):
        old = highest[group]
        new = jnp.maximum(old, jnp.max(scores, axis=0, keepdims=True))
        rescale = jnp.exp2((old - new) * factor)
        weights = jnp.exp2((scores - new) * factor)
        highest[group] = new
        totals[group] = totals[group] * rescale + jnp.sum(weights, axis=0, keepdims=True)
        weighted[group] = weighted[group] * rescale + summed(values, weights)

    def own_part(group, _):
        key_pos = lax.broadcasted_iota(jnp.int32, (rows, group_width // HEAD * rows), 0)
        query_pos = lax.rem(
            lax.broadcasted_iota(jnp.int32, (rows, group_width // HEAD * rows), 1), rows
        )
        scores = jnp.where(
            key_pos <= query_pos, scored(now_own[group, :, :HEAD], group), masked_score
        )
        new = jnp.max(scores, axis=0, keepdims=True)
        weights = jnp.exp2((scores - new) * factor)
        highest[group] = new
        totals[group] = jnp.sum(weights, axis=0, keepdims=True)
        weighted[group] = summed(now_own[group, :, HEAD:], weights)
        scores = jnp.where(
            (key_pos > query_pos) & (key_pos + me * rows >= limit),
            scored(cached_own[group, :, :HEAD], group),
            masked_score,
        )
        absorb(scores, cached_own[group, :, HEAD:], group)
        along(arrived.at[partner, group], partner, group, partner_sem.at[chip, group], partner).wait_recv()
        bound = jnp.where(partner > me, limit, 0)
        scores = jnp.where(
            key_pos + partner * rows >= bound,
            scored(arrived[partner, group, :, :HEAD], group),
            masked_score,
        )
        absorb(scores, arrived[partner, group, :, HEAD:], group)
        return 0

    lax.fori_loop(0, groups, own_part, 0)

    others = chips - 1
    both = jnp.minimum(chip, others - chip)

    def visited(step):
        shared = step < 2 * others
        group = jnp.where(shared, lax.rem(step, 2), lax.div(step, others))
        order = jnp.where(shared, lax.div(step, 2), lax.rem(step, others)) + 1
        paired = order <= 2 * both
        distance = jnp.where(paired, lax.div(order + 1, 2), order - both)
        lower = jnp.where(paired, lax.rem(order, 2) == 1, chip > both)
        return group, chip + jnp.where(lower, -distance, distance), lower, order

    def relay(step):
        group, other, lower, order = visited(step)
        owner = 2 * other + core
        block = arrived.at[owner, group]
        along(block, owner, group, chain_sem.at[other, group], partner).wait_recv()

        @pl.when(lower & (chip < chips - 1))
        def _():
            along(block, owner, group, chain_sem.at[other, group], me + 2).start()

        @pl.when(jnp.logical_not(lower) & (chip > 0))
        def _():
            along(block, owner, group, chain_sem.at[other, group], me - 2).start()

        along(block, owner, group, partner_sem.at[other, group], partner).start()

    def fold(step):
        group, other, lower, order = visited(step)
        owner = 2 * other + 1 - core
        block = arrived.at[owner, group]
        along(block, owner, group, chain_sem.at[other, group], partner).wait_recv()
        first = pl.multiple_of(2 * other, 2)
        both_blocks = arrived[pl.ds(first, 2), group].reshape(2 * rows, 2 * HEAD)
        key_pos = lax.broadcasted_iota(jnp.int32, (2 * rows, 1), 0) + first * rows
        bound = jnp.where(lower, 0, limit)
        scores = jnp.where(key_pos >= bound, scored(both_blocks[:, :HEAD], group), masked_score)
        absorb(scores, both_blocks[:, HEAD:], group)

    squares[...] = jnp.zeros_like(squares)

    def closed(group):
        attended_t = (weighted[group] * (1.0 / totals[group])).astype(jnp.bfloat16).astype(jnp.float32)
        row_squares = jnp.sum(attended_t * attended_t, axis=0, keepdims=True)
        for head in range(heads_in_group):
            squares[...] += row_squares[:, head * rows : (head + 1) * rows]
        return [
            attended_t[:, head * rows : (head + 1) * rows].T for head in range(heads_in_group)
        ]

    def fold_and_send(step):
        fold(step)
        group, _, _, order = visited(step)

        @pl.when((order == others) & (group < groups - 1))
        def _():
            for head, value in enumerate(closed(group)):
                attended_own[group, :, head * HEAD : (head + 1) * HEAD] = value.astype(
                    jnp.bfloat16
                )
            attended_send(group).start()

    def one_step(step, _):
        @pl.when(step < steps)
        def _():
            relay(step)

        fold_and_send(step - AHEAD)
        return 0

    steps = groups * others
    for step in range(AHEAD):
        relay(step)
    lax.fori_loop(AHEAD, steps + AHEAD - 1, one_step, 0)
    fold(steps - 1)

    last = closed(groups - 1)
    row_scale = lax.rsqrt(squares[...] * (1.0 / width) + EPS)
    scale_own[...] = jnp.broadcast_to(row_scale, scale_own.shape)
    scale_send.start()
    row_scale = jnp.broadcast_to(row_scale, (HEAD, rows)).T
    for head, value in enumerate(last):
        columns = slice(early + head * HEAD, early + (head + 1) * HEAD)
        branch = value * row_scale * out_gain[:, columns].astype(jnp.float32)
        final_own[:, head * HEAD : (head + 1) * HEAD] = (
            hidden_own[:, columns].astype(jnp.float32) + branch
        ).astype(jnp.bfloat16)
    final_send.start()

    hidden_send.wait_recv()
    gain_send.wait_recv()
    for group in range(groups - 1):
        attended_send(group).wait_recv()
    scale_send.wait_recv()
    row_scale = jnp.broadcast_to(scale_in[0:1, :], (HEAD, rows)).T
    for group in range(groups - 1):
        for head in range(heads_in_group):
            start = group * group_width + head * HEAD
            columns = slice(start, start + HEAD)
            branch = (
                attended_in[group, :, head * HEAD : (head + 1) * HEAD].astype(jnp.float32)
                * row_scale
                * gain_in[:, columns].astype(jnp.float32)
            )
            out_ref[:, columns] = (
                hidden_in[:, columns].astype(jnp.float32) + branch
            ).astype(jnp.bfloat16)
    final_send.wait_recv()
    out_ref[:, early:] = final_in[...]

    hidden_send.wait_send()
    gain_send.wait_send()
    scale_send.wait_send()
    final_send.wait_send()
    for group in range(groups - 1):
        attended_send(group).wait_send()

    def drained(step, _):
        group, other, lower, order = visited(step)
        owner = 2 * other + core
        block = arrived.at[owner, group]

        @pl.when((lower & (chip < chips - 1)) | (jnp.logical_not(lower) & (chip > 0)))
        def _():
            along(block, owner, group, chain_sem.at[other, group], partner).wait_send()

        along(block, owner, group, partner_sem.at[other, group], partner).wait_send()
        return 0

    lax.fori_loop(0, steps, drained, 0)
    for group in range(groups):

        @pl.when(chip < chips - 1)
        def _():
            along(now_own.at[group], me, group, chain_sem.at[chip, group], partner).wait_send()

        @pl.when(chip > 0)
        def _():
            along(cached_own.at[group], me, group, chain_sem.at[chips, group], partner).wait_send()

        along(now_own.at[group], me, group, partner_sem.at[chip, group], partner).wait_send()


def solution(mesh):
    sections, seq_count = mesh.shape["section"], mesh.shape["seq"]

    def on_device(
        hidden, query_gain, out_gain, keys_now, values_now, keys_cached, values_cached, first_key
    ):
        _, rows, width = hidden.shape
        groups = keys_now.shape[-1] // HEAD
        group_width = width // groups
        query_rows = group_width // HEAD * rows
        chips = seq_count // 2
        half, full = jnp.bfloat16, jnp.float32
        arrived_bytes = seq_count * rows * keys_now.shape[-1] * 4
        anywhere = pl.BlockSpec(memory_space=pl.ANY)
        result = pl.pallas_call(
            functools.partial(kernel, sections, seq_count, groups),
            out_shape=jax.ShapeDtypeStruct((rows, width), half),
            in_specs=[pl.BlockSpec(memory_space=pltpu.SMEM)] + [anywhere] * 7,
            out_specs=pl.BlockSpec(memory_space=pltpu.VMEM),
            scratch_shapes=[
                pltpu.VMEM((groups, rows, 2 * HEAD), half),
                pltpu.VMEM((groups, rows, 2 * HEAD), half),
                pltpu.VMEM((seq_count, groups, rows, 2 * HEAD), half),
                pltpu.VMEM((rows, width), half),
                pltpu.VMEM((1, width), half),
                pltpu.VMEM((1, width), half),
                pltpu.VMEM((groups, HEAD, query_rows), half),
                pltpu.VMEM((groups, 1, query_rows), full),
                pltpu.VMEM((groups, 1, query_rows), full),
                pltpu.VMEM((groups, HEAD, query_rows), full),
                pltpu.VMEM((groups - 1, rows, group_width), half),
                pltpu.VMEM((rows, group_width), half),
                pltpu.VMEM((8, rows), full),
                pltpu.VMEM((rows, width - group_width), half),
                pltpu.VMEM((1, width), half),
                pltpu.VMEM((groups - 1, rows, group_width), half),
                pltpu.VMEM((rows, group_width), half),
                pltpu.VMEM((8, rows), full),
                pltpu.VMEM((1, rows), full),
                pltpu.SemaphoreType.DMA((3 + 4 * groups,)),
                pltpu.SemaphoreType.DMA((seq_count, groups)),
                pltpu.SemaphoreType.DMA((chips + 1, groups)),
                pltpu.SemaphoreType.DMA((chips, groups)),
                pltpu.SemaphoreType.DMA((groups + 3,)),
                pltpu.SemaphoreType.DMA((groups + 3,)),
            ],
            compiler_params=pltpu.CompilerParams(collective_id=0, has_side_effects=True, vmem_limit_bytes=arrived_bytes + ROOM),
        )(
            first_key,
            *(
                pltpu.with_memory_space_constraint(value, pltpu.HBM)
                for value in (
                    hidden[0],
                    query_gain,
                    out_gain,
                    keys_now[0],
                    values_now[0],
                    keys_cached[0],
                    values_cached[0],
                )
            ),
        )
        return result[None]

    return jax.shard_map(
        on_device,
        mesh=mesh,
        in_specs=(
            P("section", "seq", None),
            P("section", None),
            P("section", None),
            P("section", "seq", None),
            P("section", "seq", None),
            P("section", "seq", None),
            P("section", "seq", None),
            P("section"),
        ),
        out_specs=P("section", "seq", None),
        check_vma=False,
    )
```

```python
import functools
import math

import jax
import jax.numpy as jnp
from jax import lax
from jax.experimental import pallas as pl
from jax.experimental.pallas import tpu as pltpu
from jax.sharding import PartitionSpec as P

HEAD = 128
EPS = 1e-06
AHEAD = 2
ROOM = 20 << 20
masked_score = -1e30
MESH = pl.DeviceIdType.MESH


def kernel(
    sections,
    seq_count,
    groups,
    first_key_ref,
    hidden_ref,
    query_gain_ref,
    out_gain_ref,
    keys_now_ref,
    values_now_ref,
    keys_cached_ref,
    values_cached_ref,
    out_ref,
    now_own,
    cached_own,
    arrived,
    hidden_own,
    query_gain,
    out_gain,
    queries_t,
    highest,
    totals,
    weighted,
    attended_own,
    final_own,
    scale_own,
    hidden_in,
    gain_in,
    attended_in,
    final_in,
    scale_in,
    squares,
    local_sem,
    arrive_sem,
    chain_sem,
    partner_sem,
    section_send,
    section_recv,
):
    rows, width = hidden_ref.shape
    group_width = width // groups
    heads_in_group = group_width // HEAD
    chips = seq_count // 2
    early = group_width * (groups - 1)
    factor = math.log2(math.e) * HEAD ** (-0.5)
    section = lax.axis_index("section")
    me = lax.axis_index("seq")
    chip = lax.div(me, 2)
    core = lax.rem(me, 2)
    partner = me + 1 - 2 * core
    next_section = lax.rem(section + 1, sections)
    last_section = lax.rem(section + sections - 1, sections)
    limit = first_key_ref[0]

    barrier = pltpu.get_barrier_semaphore()

    def greet(section_id, seq_id):
        pl.semaphore_signal(barrier, inc=1, device_id=(section_id, seq_id), device_id_type=MESH)

    greet(section, partner)
    greet(next_section, me)
    greet(last_section, me)

    @pl.when(chip > 0)
    def _():
        greet(section, me - 2)

    @pl.when(chip < chips - 1)
    def _():
        greet(section, me + 2)

    hidden_copy = pltpu.make_async_copy(hidden_ref, hidden_own, local_sem.at[0])
    gain_copy = pltpu.make_async_copy(query_gain_ref, query_gain, local_sem.at[1])
    out_gain_copy = pltpu.make_async_copy(out_gain_ref, out_gain, local_sem.at[2])
    pieces = []
    for group in range(groups):
        columns = pl.ds(group * HEAD, HEAD)
        pieces.append(
            [
                pltpu.make_async_copy(
                    source.at[:, columns],
                    packed.at[group, :, pl.ds(half * HEAD, HEAD)],
                    local_sem.at[3 + 4 * group + number],
                )
                for number, (source, packed, half) in enumerate(
                    (
                        (keys_now_ref, now_own, 0),
                        (values_now_ref, now_own, 1),
                        (keys_cached_ref, cached_own, 0),
                        (values_cached_ref, cached_own, 1),
                    )
                )
            ]
        )
    for copy in pieces[0]:
        copy.start()
    hidden_copy.start()
    gain_copy.start()
    out_gain_copy.start()
    for group in range(1, groups):
        for copy in pieces[group]:
            copy.start()

    ends = (chip == 0).astype(jnp.int32) + (chip == chips - 1).astype(jnp.int32)
    pl.semaphore_wait(barrier, 5 - ends)

    def along(source, owner, group, send_sem, target):
        return pltpu.make_async_remote_copy(
            src_ref=source,
            dst_ref=arrived.at[owner, group],
            send_sem=send_sem,
            recv_sem=arrive_sem.at[owner, group],
            device_id=(section, target),
            device_id_type=MESH,
        )

    def to_next(source, target, number):
        return pltpu.make_async_remote_copy(
            src_ref=source,
            dst_ref=target,
            send_sem=section_send.at[number],
            recv_sem=section_recv.at[number],
            device_id=(next_section, me),
            device_id_type=MESH,
        )

    hidden_send = to_next(hidden_ref.at[:, pl.ds(0, early)], hidden_in, groups - 1)
    gain_send = to_next(out_gain, gain_in, groups)
    scale_send = to_next(scale_own, scale_in, groups + 1)

    def final_send(head):
        return to_next(final_own.at[head], final_in.at[head], groups + 2 + head)

    def attended_send(group):
        return to_next(attended_own.at[group], attended_in.at[group], group)

    for group in range(groups):
        for copy in pieces[group]:
            copy.wait()

        @pl.when(chip < chips - 1)
        def _():
            along(now_own.at[group], me, group, chain_sem.at[chip, group], me + 2).start()

        @pl.when(chip > 0)
        def _():
            along(cached_own.at[group], me, group, chain_sem.at[chips, group], me - 2).start()

        @pl.when(core == 0)
        def _():
            along(now_own.at[group], me, group, partner_sem.at[chip, group], partner).start()

        @pl.when(core == 1)
        def _():
            along(cached_own.at[group], me, group, partner_sem.at[chip, group], partner).start()

        if group == 0:
            hidden_send.start()
            out_gain_copy.wait()
            gain_send.start()

    hidden_copy.wait()
    gain_copy.wait()
    widened = hidden_own[...].astype(jnp.float32)
    scale = lax.rsqrt(jnp.mean(widened * widened, axis=-1, keepdims=True) + EPS)
    for head in range(groups * heads_in_group):
        columns = slice(head * HEAD, (head + 1) * HEAD)
        queries = (
            hidden_own[:, columns].astype(jnp.float32)
            * scale
            * query_gain[:, columns].astype(jnp.float32)
        )
        place = head % heads_in_group
        queries_t[head // heads_in_group, :, place * rows : (place + 1) * rows] = (
            queries.T.astype(jnp.bfloat16)
        )

    def scored(keys, group):
        return jnp.dot(keys, queries_t[group], preferred_element_type=jnp.float32)

    def summed(values, weights):
        return lax.dot_general(
            values,
            weights.astype(jnp.bfloat16),
            (((0,), (0,)), ((), ())),
            preferred_element_type=jnp.float32,
        )

    def absorb(scores, values, group):
        old = highest[group]
        new = jnp.maximum(old, jnp.max(scores, axis=0, keepdims=True))
        rescale = jnp.exp2((old - new) * factor)
        weights = jnp.exp2((scores - new) * factor)
        highest[group] = new
        totals[group] = totals[group] * rescale + jnp.sum(weights, axis=0, keepdims=True)
        weighted[group] = weighted[group] * rescale + summed(values, weights)

    def own_part(group, _):
        key_pos = lax.broadcasted_iota(jnp.int32, (rows, group_width // HEAD * rows), 0)
        query_pos = lax.rem(
            lax.broadcasted_iota(jnp.int32, (rows, group_width // HEAD * rows), 1), rows
        )
        scores = jnp.where(
            key_pos <= query_pos, scored(now_own[group, :, :HEAD], group), masked_score
        )
        new = jnp.max(scores, axis=0, keepdims=True)
        weights = jnp.exp2((scores - new) * factor)
        highest[group] = new
        totals[group] = jnp.sum(weights, axis=0, keepdims=True)
        weighted[group] = summed(now_own[group, :, HEAD:], weights)
        scores = jnp.where(
            (key_pos > query_pos) & (key_pos + me * rows >= limit),
            scored(cached_own[group, :, :HEAD], group),
            masked_score,
        )
        absorb(scores, cached_own[group, :, HEAD:], group)
        along(arrived.at[partner, group], partner, group, partner_sem.at[chip, group], partner).wait_recv()
        bound = jnp.where(partner > me, limit, 0)
        scores = jnp.where(
            key_pos + partner * rows >= bound,
            scored(arrived[partner, group, :, :HEAD], group),
            masked_score,
        )
        absorb(scores, arrived[partner, group, :, HEAD:], group)
        return 0

    lax.fori_loop(0, groups, own_part, 0)

    others = chips - 1
    both = jnp.minimum(chip, others - chip)

    def visited(step):
        shared = step < 2 * others
        group = jnp.where(shared, lax.rem(step, 2), lax.div(step, others))
        order = jnp.where(shared, lax.div(step, 2), lax.rem(step, others)) + 1
        paired = order <= 2 * both
        distance = jnp.where(paired, lax.div(order + 1, 2), order - both)
        lower = jnp.where(paired, lax.rem(order, 2) == 1, chip > both)
        return group, chip + jnp.where(lower, -distance, distance), lower, order

    def relay(step):
        group, other, lower, order = visited(step)
        owner = 2 * other + core
        block = arrived.at[owner, group]
        along(block, owner, group, chain_sem.at[other, group], partner).wait_recv()

        @pl.when(lower & (chip < chips - 1))
        def _():
            along(block, owner, group, chain_sem.at[other, group], me + 2).start()

        @pl.when(jnp.logical_not(lower) & (chip > 0))
        def _():
            along(block, owner, group, chain_sem.at[other, group], me - 2).start()

        along(block, owner, group, partner_sem.at[other, group], partner).start()

    def fold(step):
        group, other, lower, order = visited(step)
        owner = 2 * other + 1 - core
        block = arrived.at[owner, group]
        along(block, owner, group, chain_sem.at[other, group], partner).wait_recv()
        first = pl.multiple_of(2 * other, 2)
        both_blocks = arrived[pl.ds(first, 2), group].reshape(2 * rows, 2 * HEAD)
        key_pos = lax.broadcasted_iota(jnp.int32, (2 * rows, 1), 0) + first * rows
        bound = jnp.where(lower, 0, limit)
        scores = jnp.where(key_pos >= bound, scored(both_blocks[:, :HEAD], group), masked_score)
        absorb(scores, both_blocks[:, HEAD:], group)

    squares[...] = jnp.zeros_like(squares)

    def closed(group):
        attended_t = (weighted[group] * (1.0 / totals[group])).astype(jnp.bfloat16).astype(jnp.float32)
        row_squares = jnp.sum(attended_t * attended_t, axis=0, keepdims=True)
        for head in range(heads_in_group):
            squares[...] += row_squares[:, head * rows : (head + 1) * rows]
        return [
            attended_t[:, head * rows : (head + 1) * rows].T for head in range(heads_in_group)
        ]

    def fold_and_send(step):
        fold(step)
        group, _, _, order = visited(step)

        @pl.when((order == others) & (group < groups - 1))
        def _():
            for head, value in enumerate(closed(group)):
                attended_own[group, :, head * HEAD : (head + 1) * HEAD] = value.astype(
                    jnp.bfloat16
                )
            attended_send(group).start()

    def one_step(step, _):
        @pl.when(step < steps)
        def _():
            relay(step)

        fold_and_send(step - AHEAD)
        return 0

    steps = groups * others
    for step in range(AHEAD):
        relay(step)
    lax.fori_loop(AHEAD, steps + AHEAD - 1, one_step, 0)
    fold(steps - 1)

    last = closed(groups - 1)
    row_scale = lax.rsqrt(squares[...] * (1.0 / width) + EPS)
    scale_own[...] = jnp.broadcast_to(row_scale, scale_own.shape)
    scale_send.start()
    row_scale = jnp.broadcast_to(row_scale, (HEAD, rows)).T
    for head, value in enumerate(last):
        columns = slice(early + head * HEAD, early + (head + 1) * HEAD)
        branch = value * row_scale * out_gain[:, columns].astype(jnp.float32)
        final_own[head] = (
            hidden_own[:, columns].astype(jnp.float32) + branch
        ).astype(jnp.bfloat16)
        final_send(head).start()

    hidden_send.wait_recv()
    gain_send.wait_recv()
    for group in range(groups - 1):
        attended_send(group).wait_recv()
    scale_send.wait_recv()
    row_scale = jnp.broadcast_to(scale_in[0:1, :], (HEAD, rows)).T
    for group in range(groups - 1):
        for head in range(heads_in_group):
            start = group * group_width + head * HEAD
            columns = slice(start, start + HEAD)
            branch = (
                attended_in[group, :, head * HEAD : (head + 1) * HEAD].astype(jnp.float32)
                * row_scale
                * gain_in[:, columns].astype(jnp.float32)
            )
            out_ref[:, columns] = (
                hidden_in[:, columns].astype(jnp.float32) + branch
            ).astype(jnp.bfloat16)
    hidden_send.wait_send()
    gain_send.wait_send()
    scale_send.wait_send()
    for group in range(groups - 1):
        attended_send(group).wait_send()

    def drained(step, _):
        group, other, lower, order = visited(step)
        owner = 2 * other + core
        block = arrived.at[owner, group]

        @pl.when((lower & (chip < chips - 1)) | (jnp.logical_not(lower) & (chip > 0)))
        def _():
            along(block, owner, group, chain_sem.at[other, group], partner).wait_send()

        along(block, owner, group, partner_sem.at[other, group], partner).wait_send()
        return 0

    lax.fori_loop(0, steps, drained, 0)
    for group in range(groups):

        @pl.when(chip < chips - 1)
        def _():
            along(now_own.at[group], me, group, chain_sem.at[chip, group], partner).wait_send()

        @pl.when(chip > 0)
        def _():
            along(cached_own.at[group], me, group, chain_sem.at[chips, group], partner).wait_send()

        along(now_own.at[group], me, group, partner_sem.at[chip, group], partner).wait_send()

    for head in range(heads_in_group):
        final_send(head).wait_recv()
        out_ref[:, early + head * HEAD : early + (head + 1) * HEAD] = final_in[head]
    for head in range(heads_in_group):
        final_send(head).wait_send()


def solution(mesh):
    sections, seq_count = mesh.shape["section"], mesh.shape["seq"]

    def on_device(
        hidden, query_gain, out_gain, keys_now, values_now, keys_cached, values_cached, first_key
    ):
        _, rows, width = hidden.shape
        groups = keys_now.shape[-1] // HEAD
        group_width = width // groups
        query_rows = group_width // HEAD * rows
        chips = seq_count // 2
        half, full = jnp.bfloat16, jnp.float32
        arrived_bytes = seq_count * rows * keys_now.shape[-1] * 4
        anywhere = pl.BlockSpec(memory_space=pl.ANY)
        result = pl.pallas_call(
            functools.partial(kernel, sections, seq_count, groups),
            out_shape=jax.ShapeDtypeStruct((rows, width), half),
            in_specs=[pl.BlockSpec(memory_space=pltpu.SMEM)] + [anywhere] * 7,
            out_specs=pl.BlockSpec(memory_space=pltpu.VMEM),
            scratch_shapes=[
                pltpu.VMEM((groups, rows, 2 * HEAD), half),
                pltpu.VMEM((groups, rows, 2 * HEAD), half),
                pltpu.VMEM((seq_count, groups, rows, 2 * HEAD), half),
                pltpu.VMEM((rows, width), half),
                pltpu.VMEM((1, width), half),
                pltpu.VMEM((1, width), half),
                pltpu.VMEM((groups, HEAD, query_rows), half),
                pltpu.VMEM((groups, 1, query_rows), full),
                pltpu.VMEM((groups, 1, query_rows), full),
                pltpu.VMEM((groups, HEAD, query_rows), full),
                pltpu.VMEM((groups - 1, rows, group_width), half),
                pltpu.VMEM((group_width // HEAD, rows, HEAD), half),
                pltpu.VMEM((8, rows), full),
                pltpu.VMEM((rows, width - group_width), half),
                pltpu.VMEM((1, width), half),
                pltpu.VMEM((groups - 1, rows, group_width), half),
                pltpu.VMEM((group_width // HEAD, rows, HEAD), half),
                pltpu.VMEM((8, rows), full),
                pltpu.VMEM((1, rows), full),
                pltpu.SemaphoreType.DMA((3 + 4 * groups,)),
                pltpu.SemaphoreType.DMA((seq_count, groups)),
                pltpu.SemaphoreType.DMA((chips + 1, groups)),
                pltpu.SemaphoreType.DMA((chips, groups)),
                pltpu.SemaphoreType.DMA((groups + 2 + group_width // HEAD,)),
                pltpu.SemaphoreType.DMA((groups + 2 + group_width // HEAD,)),
            ],
            compiler_params=pltpu.CompilerParams(collective_id=0, has_side_effects=True, vmem_limit_bytes=arrived_bytes + ROOM),
        )(
            first_key,
            *(
                pltpu.with_memory_space_constraint(value, pltpu.HBM)
                for value in (
                    hidden[0],
                    query_gain,
                    out_gain,
                    keys_now[0],
                    values_now[0],
                    keys_cached[0],
                    values_cached[0],
                )
            ),
        )
        return result[None]

    return jax.shard_map(
        on_device,
        mesh=mesh,
        in_specs=(
            P("section", "seq", None),
            P("section", None),
            P("section", None),
            P("section", "seq", None),
            P("section", "seq", None),
            P("section", "seq", None),
            P("section", "seq", None),
            P("section"),
        ),
        out_specs=P("section", "seq", None),
        check_vma=False,
    )
```
